32 devices in a mesh: lon: 8 (over z, x), lat: 4 (over y, core).
Axes of the slice: x: 2, y: 2, z: 4, core: 2. Of those that a mesh axis runs over, the one named last changes fastest.
Arguments:
- kappa_east: float32 [64, 1024], P('lat', 'lon'), may hold values from 0.02 to 0.2
- kappa_north: float32 [64, 1024], P('lat', 'lon'), may hold values from 0.02 to 0.2
- depth: int32 [64, 1024], P('lat', 'lon'), may hold values from 0 to 75
- sigma: float32 [151], replicated, may hold values from 0.3 to 3
- obs_precision: float32 [151], replicated, may hold values from 0.5 to 4
- obs_tile: int32 [4096, 1], P(('lon', 'lat')), may hold values from 0 to 7; in each aligned block of 128 rows (0 to 127, 128 to 255, ...) at most 32 rows name the same one
- obs_col: int32 [4096], P(('lon', 'lat')), may hold values from 0 to 127
- obs_lat: int32 [4096], P(('lon', 'lat')), may hold values from 0 to 15
- innovation: float32 [151, 4096], P(None, ('lon', 'lat')), may hold values from -6 to 6
Outputs:
- increment: float32 [151, 64, 1024], P(None, 'lat', 'lon')
- residual: float32 [151, 64, 1024], P(None, 'lat', 'lon')
The draws below stay inside these ranges and needn't reach their ends.
Inputs may be any that keep to these rules, and one draw needn't show every extreme that they name: `obs_tile`: among the 128 profiles listed on one device, no longitude tile is named by more than 32, a bound that some block reaches.
All inputs are finite; a program needn't handle non-finite values.
Results may differ from the reference program's by a relative error of at most 0.00013.
Values sent between devices are 32-bit elements; how exact they have to be, the bound alone decides.
A program may use at most 128 MiB of HBM per device.

```python
import math
import jax
import jax.numpy as jnp
import numpy as np

NZ = 75
CX = 128
CY = 16
OBS_DEV = 128
ITERS = 2
CH = 151
NX = 1024
NY = 64
NOBS = 4096
CAP = 32
N_LON = 8
N_LAT = 4


def set_ends(values, own_key, least, largest):
    longest = values.shape.index(max(values.shape))
    spots = []
    for shift in (0, 1):
        where = [jax.random.randint(jax.random.fold_in(own_key, axis), (), 0, length) for axis, length in enumerate(values.shape)]
        where[longest] = (where[longest] + shift) % values.shape[longest]
        spots.append(tuple(where))
    return values.at[spots[0]].set(least).at[spots[1]].set(largest)


def shard_levels(key, shape, shards, smallest, top_value):
    level, own = 1.0, jax.random.fold_in(key, 6)
    for dim, shards_of in shards:
        draws = jnp.exp(jax.random.uniform(jax.random.fold_in(own, dim), (shards_of,), jnp.float32, smallest / len(shards), top_value / len(shards)))
        level = level * jnp.repeat(draws, shape[dim] // shards_of).reshape([-1 if axis == dim else 1 for axis in range(len(shape))])
    return level


def routed_block(key, own, number, rows, amount, top, limit, skew):
    ranking = jax.random.permutation(key, amount)
    heavy_load, common = load_shares(amount, rows * top, limit, skew, True), load_shares(amount, rows * top, limit, skew, False)
    places = jnp.arange(amount)

    def named(lengths, offset_by):
        used = int((lengths > 0).sum())
        fixed = max(1, used // 4)
        shifted = fixed + (places - fixed + offset_by * (used - fixed)) % max(1, amount - fixed)
        return jnp.zeros((amount,), jnp.int32).at[ranking[jnp.where(places < fixed, places, shifted)]].set(jnp.asarray(lengths, jnp.int32))

    lengths = jnp.where(number % 4 == 0, named(heavy_load, number // 4), named(common, number - number // 4 - 1))
    mixed = jax.random.permutation(jax.random.fold_in(own, 3), amount)
    donor, receiver = mixed[0:amount // 2 * 2:2], mixed[1:amount // 2 * 2:2]
    room = jnp.minimum(lengths[donor] - 1, limit - lengths[receiver]) // 2
    room = jnp.where((donor == ranking[0]) | (receiver == ranking[0]) | (lengths[receiver] == 0), 0, jnp.maximum(room, 0))
    shifted = jax.random.randint(jax.random.fold_in(own, 4), (amount // 2,), 0, 1 << 20) % (room + 1)
    lengths = lengths.at[donor].add(-shifted).at[receiver].add(shifted)
    labels = jnp.searchsorted(jnp.cumsum(lengths), jnp.arange(rows * top), side="right").astype(jnp.int32)
    listing = labels.reshape(top, rows).T
    listing = listing[jax.random.permutation(jax.random.fold_in(own, 1), rows)]
    offset_by = jax.random.randint(jax.random.fold_in(own, 2), (rows, 1), 0, top)
    return jnp.take_along_axis(listing, (jnp.arange(top)[None, :] + offset_by) % top, axis=1)


def load_shares(count, total, limit, skew, full):
    weights = [(1 << 20) // math.isqrt(standing ** skew) + 1 for standing in range(1, count + 1)]
    largest = limit if full else min(limit, max(-(-total // count), total * weights[0] // sum(weights)))
    least = 1 if total - largest >= count - 1 else 0
    holding, surplus = [largest] + [least] * (count - 1), total - largest - least * (count - 1)
    while surplus > 0:
        movable = [i for i in range(1, count) if holding[i] < largest] or [i for i in range(1, count) if holding[i] < limit]
        whole, budget = sum([weights[i] for i in movable]), surplus
        for i in movable:
            more = min(limit - holding[i], max(1, budget * weights[i] // whole), surplus)
            holding[i] = holding[i] + more
            surplus = surplus - more
    return np.array(holding)


def scatter_about(stream_key, shape, spread, reach, shards=(), kind=jnp.bfloat16):
    array = spread * jax.random.normal(stream_key, shape, jnp.float32)
    if shards:
        array = array * shard_levels(stream_key, shape, shards, -0.22, 0.18)
    return jnp.clip(array, -reach, reach).astype(kind)


def setup_inputs(seed: int = 0) -> dict:
    seeds = jax.random.split(jax.random.key(seed), 10)
    kappa_east = jnp.clip(0.02 + 0.18 * jax.random.uniform(seeds[0], (NY, NX), jnp.float32) ** shard_levels(seeds[0], (NY, NX), ((0, 4), (1, 8)), -0.2, 0.2), 0.02, 0.2)
    kappa_north = jnp.clip(0.02 + 0.18 * jax.random.uniform(seeds[1], (NY, NX), jnp.float32) ** shard_levels(seeds[1], (NY, NX), ((0, 4), (1, 8)), -0.2, 0.2), 0.02, 0.2)
    depth = set_ends(jax.random.randint(seeds[2], (NY, NX), 0, NZ + 1), jax.random.fold_in(seeds[2], 1), 0, NZ).astype(jnp.int32)
    sigma = jnp.clip(jnp.exp(jax.random.uniform(seeds[3], (CH,), jnp.float32, math.log(0.3), math.log(3.0))), 0.3, 3.0)
    obs_precision = jnp.clip(jnp.exp(jax.random.uniform(seeds[4], (CH,), jnp.float32, math.log(0.5), math.log(4.0))), 0.5, 4.0)
    obs_tile_keys = jax.random.split(jax.random.fold_in(seeds[5], 1), NOBS // OBS_DEV)
    obs_tile_turns = jax.random.permutation(jax.random.fold_in(seeds[5], 3), NOBS // OBS_DEV)
    obs_tile = jax.vmap(lambda own, number: routed_block(jax.random.fold_in(seeds[5], 2), own, number, OBS_DEV, N_LON, 1, CAP, 0))(obs_tile_keys, obs_tile_turns).reshape((NOBS, 1))
    obs_col = set_ends(jax.random.randint(seeds[6], (NOBS,), 0, CX), jax.random.fold_in(seeds[6], 1), 0, CX - 1).astype(jnp.int32)
    obs_lat = set_ends(jax.random.randint(seeds[7], (NOBS,), 0, CY), jax.random.fold_in(seeds[7], 1), 0, CY - 1).astype(jnp.int32)
    innovation = scatter_about(seeds[8], (CH, NOBS), 1.0, 6.0, ((1, 32),), jnp.float32)
    return dict(kappa_east=kappa_east, kappa_north=kappa_north, depth=depth, sigma=sigma, obs_precision=obs_precision, obs_tile=obs_tile, obs_col=obs_col, obs_lat=obs_lat, innovation=innovation)


def smooth_once(v, face_east, face_north):
    east = jnp.roll(v, -1, 2)
    west = jnp.roll(v, 1, 2)
    north = jnp.roll(v, -1, 1)
    south = jnp.roll(v, 1, 1)
    out = v + face_east * (east - v) + jnp.roll(face_east, 1, 2) * (west - v)
    return out + face_north * (north - v) + jnp.roll(face_north, 1, 1) * (south - v)


def smooth_five(v, face_east, face_north):
    for step in range(5):
        v = smooth_once(v, face_east, face_north)
    return v


def reference(kappa_east, kappa_north, depth, sigma, obs_precision, obs_tile, obs_col, obs_lat, innovation):
    levels = jnp.arange(CH, dtype=jnp.int32)
    level_of = jnp.where(levels < 2 * NZ, levels % NZ, 0).astype(jnp.int32)
    wet = (depth[None, :, :] > level_of[:, None, None]).astype(jnp.float32)
    keep_row = (jnp.arange(NY, dtype=jnp.int32) < NY - 1).astype(jnp.float32)[:, None]
    face_east = kappa_east[None] * wet * jnp.roll(wet, -1, 2)
    face_north = (kappa_north * keep_row)[None] * wet * jnp.roll(wet, -1, 1)
    order = jnp.arange(NOBS, dtype=jnp.int32)
    obs_row = ((order // OBS_DEV) % N_LAT) * CY + obs_lat
    obs_lon = (obs_tile[:, 0] * CX + obs_col).astype(jnp.int32)
    scale = sigma[:, None, None]
    weight = obs_precision[:, None]

    def forward_obs(u):
        return (u * wet)[:, obs_row, obs_lon]

    def adjoint_obs(w):
        cells = jnp.zeros((CH, NY, NX), jnp.float32).at[:, obs_row, obs_lon].add(w)
        return cells * wet

    def hessian(p):
        u = scale * smooth_five(p, face_east, face_north)
        w = weight * forward_obs(u)
        return p + smooth_five(scale * adjoint_obs(w), face_east, face_north)

    rhs = smooth_five(scale * adjoint_obs(weight * innovation), face_east, face_north)
    increment = jnp.zeros_like(rhs)
    residual = rhs
    direction = rhs
    norm_now = jnp.sum(residual * residual)
    for step in range(ITERS):
        image = hessian(direction)
        alpha = norm_now / jnp.sum(direction * image)
        increment = increment + alpha * direction
        residual = residual - alpha * image
        norm_next = jnp.sum(residual * residual)
        direction = residual + (norm_next / norm_now) * direction
        norm_now = norm_next
    return increment, residual
```

```python
import functools

import jax
import jax.numpy as jnp
from jax import lax
from jax.experimental import pallas as pl
from jax.experimental.pallas import tpu as pltpu
from jax.sharding import PartitionSpec as P

NZ = 75
AXES = ("lon", "lat")


def smooth_kernel(lev, x, ke, kw, kn, de, dw, dn, *rest):
    if len(rest) == 8:
        gain, out, va, vb, fe, fw, fn, dd = rest
    else:
        gain = None
        out, va, vb, fe, fw, fn, dd = rest
    channels, rows, tiles, lanes = x.shape
    block = 8
    blocks = rows // block
    zero = jnp.zeros((tiles, lanes), jnp.float32)
    for c in range(channels):
        va[c, 0] = zero
        vb[c, 0] = zero
        va[c, rows + 1] = zero
        vb[c, rows + 1] = zero
        fn[c, 0] = zero

    def build(i, carry):
        c = i // blocks
        r = (i % blocks) * block
        here = pl.ds(r, block)
        level = lev[c]
        east = jnp.where(de[here] > level, ke[here], 0.0)
        west = jnp.where(dw[here] > level, kw[here], 0.0)
        north = jnp.where(dn[here] > level, kn[here], 0.0)
        fe[c, here] = east
        fw[c, here] = west
        fn[c, pl.ds(r + 1, block)] = north
        south = fn[c, here]
        dd[c, here] = 1.0 - (east + west + north + south)
        cells = x[c, here]
        if gain is not None:
            cells = cells * gain[c, here]
        va[c, pl.ds(r + 1, block)] = cells
        return carry

    lax.fori_loop(0, channels * blocks, build, 0)
    lane = lax.broadcasted_iota(jnp.int32, (block, tiles, lanes), 2)

    def step(src, dst, shift):
        def body(i, carry):
            c = i // blocks
            r = (i % blocks) * block
            here = pl.ds(r, block)
            centre = src[c, pl.ds(r + 1, block)]
            east = pltpu.roll(centre, lanes - 1, 2)
            east = jnp.where(lane == lanes - 1, pltpu.roll(east, tiles - 1, 1), east)
            west = pltpu.roll(centre, 1, 2)
            west = jnp.where(lane == 0, pltpu.roll(west, 1, 1), west)
            new = dd[c, here] * centre + fe[c, here] * east + fw[c, here] * west
            new = new + fn[c, pl.ds(r + 1, block)] * src[c, pl.ds(r + 2, block)]
            new = new + fn[c, here] * src[c, here]
            dst[c, pl.ds(r + shift, block)] = new
            return carry

        lax.fori_loop(0, channels * blocks, body, 0)

    step(va, vb, 1)
    step(vb, va, 1)
    step(va, vb, 1)
    step(vb, va, 1)
    step(va, out, 0)


def smooth_five(x, faces, lev, gain=None):
    channels, rows, tiles, lanes = x.shape
    vmem = pl.BlockSpec(memory_space=pltpu.VMEM)
    operands = [lev, x, *faces] + ([] if gain is None else [gain])
    field = pltpu.VMEM((channels, rows, tiles, lanes), jnp.float32)
    padded = pltpu.VMEM((channels, rows + 2, tiles, lanes), jnp.float32)
    cells = channels * rows * tiles * lanes
    return pl.pallas_call(
        smooth_kernel,
        out_shape=jax.ShapeDtypeStruct(x.shape, jnp.float32),
        in_specs=[pl.BlockSpec(memory_space=pltpu.SMEM)] + [vmem] * (len(operands) - 1),
        out_specs=vmem,
        scratch_shapes=[padded, padded, field, field, padded, field],
        cost_estimate=pl.CostEstimate(
            flops=60 * cells, bytes_accessed=16 * cells, transcendentals=0
        ),
        compiler_params=pltpu.CompilerParams(vmem_limit_bytes=48 * 1024 * 1024),
        name="smooth_five",
    )(*operands)


def local(
    kappa_east, kappa_north, depth, sigma, obs_precision, obs_tile, obs_col, obs_lat, innovation
):
    rows, lanes = kappa_east.shape
    total = sigma.shape[0]
    tiles = lax.axis_size("lon")
    bands = lax.axis_size("lat")
    devices = tiles * bands
    channels = -(-total // devices)
    listed = obs_col.shape[0]
    spare = channels * devices - total

    obs_lon = obs_tile[:, 0] * lanes + obs_col
    packed = jnp.concatenate(
        [
            kappa_east.reshape(-1),
            kappa_north.reshape(-1),
            depth.astype(jnp.float32).reshape(-1),
            obs_lon.astype(jnp.float32),
            obs_lat.astype(jnp.float32),
        ]
    ).reshape(-1, lanes)
    everywhere = lax.all_gather(packed, AXES, axis=0, tiled=False)
    maps = everywhere[:, : 3 * rows].reshape(tiles, bands, 3, rows, lanes)
    maps = maps.transpose(2, 1, 3, 0, 4).reshape(3, bands * rows, tiles, lanes)
    places = everywhere[:, 3 * rows :].reshape(tiles, bands, 2, listed)
    places = places.transpose(2, 1, 0, 3).reshape(2, bands, tiles * listed)

    misfit = jnp.pad(obs_precision[:, None] * innovation, ((0, spare), (0, 0)))
    misfit = lax.all_to_all(
        misfit.reshape(devices, channels, listed), AXES, split_axis=0, concat_axis=0, tiled=True
    )
    misfit = misfit.reshape(tiles, bands, channels, listed).transpose(1, 2, 0, 3)
    misfit = misfit.reshape(bands, channels, tiles * listed)

    me = lax.axis_index("lon") * bands + lax.axis_index("lat")
    first = me * channels
    ids = first + jnp.arange(channels, dtype=jnp.int32)
    lev = jnp.where(ids < 2 * NZ, ids % NZ, 0).astype(jnp.float32)
    scale = lax.dynamic_slice(jnp.pad(sigma, (0, spare)), (first,), (channels,))
    weight = lax.dynamic_slice(jnp.pad(obs_precision, (0, spare)), (first,), (channels,))

    height = bands * rows
    ke, kn, deep = maps[0], maps[1], maps[2]

    def shifted(field, by):
        flat = field.reshape(height, tiles * lanes)
        return jnp.roll(flat, by, 1).reshape(field.shape)

    kept = (jnp.arange(height) < height - 1)[:, None, None]
    kn = jnp.where(kept, kn, 0.0)
    de = jnp.minimum(deep, shifted(deep, -1))
    faces = (
        ke,
        shifted(ke, 1),
        kn,
        de,
        shifted(de, 1),
        jnp.minimum(deep, jnp.roll(deep, -1, 0)),
    )

    values = jnp.concatenate([misfit, jnp.ones_like(misfit[:, :1])], axis=1)
    high = lax.reduce_precision(values, 8, 7)
    left = values - high
    middle = lax.reduce_precision(left, 8, 7)
    low = left - middle
    parts = jnp.stack([high, middle, low], axis=1).astype(jnp.bfloat16)
    at_row = places[1][:, None, :] == jnp.arange(rows, dtype=jnp.float32)[None, :, None]
    at_col = (
        places[0][:, None, :] == jnp.arange(tiles * lanes, dtype=jnp.float32)[None, :, None]
    )
    spread = jnp.where(at_row[:, None, None], parts[:, :, :, None, :], 0)
    spread = spread.reshape(bands, 3 * (channels + 1) * rows, tiles * listed)
    cells = lax.dot_general(
        spread,
        at_col.astype(jnp.bfloat16),
        (((2,), (2,)), ((0,), (0,))),
        preferred_element_type=jnp.float32,
    )
    cells = cells.reshape(bands, 3, channels + 1, rows, tiles, lanes).sum(1)
    cells = cells.transpose(1, 0, 2, 3, 4).reshape(channels + 1, height, tiles, lanes)
    wet = (deep[None] > lev[:, None, None, None]).astype(jnp.float32)
    scaled_wet = scale[:, None, None, None] * wet
    gain = scaled_wet * (scale * weight)[:, None, None, None] * cells[channels][None]

    rhs = smooth_five(scaled_wet * cells[:channels], faces, lev)
    q_one = smooth_five(rhs, faces, lev)
    sums = lax.psum(
        jnp.stack([jnp.sum(rhs * rhs), jnp.sum(q_one * q_one * gain)]), AXES
    )
    s_one = smooth_five(q_one, faces, lev, gain)
    norm_zero = sums[0]
    alpha_one = norm_zero / (norm_zero + sums[1])
    r_one = rhs - alpha_one * (rhs + s_one)
    norm_one = lax.psum(jnp.sum(r_one * r_one), AXES)
    t_one = smooth_five(r_one, faces, lev)
    beta = norm_one / norm_zero
    p_two = r_one + beta * rhs
    q_two = t_one + beta * q_one
    curve = lax.psum(jnp.sum(p_two * p_two + q_two * q_two * gain), AXES)
    s_two = smooth_five(q_two, faces, lev, gain)
    alpha_two = norm_one / curve

    def home(field):
        split = field.reshape(channels, bands, rows, tiles, lanes).transpose(3, 1, 0, 2, 4)
        split = split.reshape(devices, channels, rows, lanes)
        moved = lax.all_to_all(split, AXES, split_axis=0, concat_axis=0, tiled=True)
        return moved.reshape(devices * channels, rows, lanes)[:total]

    increment = home(alpha_one * rhs + alpha_two * p_two)
    residual = home(r_one - alpha_two * (p_two + s_two))
    return increment, residual


def solution(mesh):
    return jax.shard_map(
        local,
        mesh=mesh,
        in_specs=(
            P("lat", "lon"),
            P("lat", "lon"),
            P("lat", "lon"),
            P(),
            P(),
            P(("lon", "lat"), None),
            P(("lon", "lat")),
            P(("lon", "lat")),
            P(None, ("lon", "lat")),
        ),
        out_specs=(P(None, "lat", "lon"), P(None, "lat", "lon")),
        check_vma=False,
    )
```

```python
import functools

import jax
import jax.numpy as jnp
from jax import lax
from jax.experimental import pallas as pl
from jax.experimental.pallas import tpu as pltpu
from jax.sharding import PartitionSpec as P

NZ = 75
AXES = ("lon", "lat")
BLOCK = 64


def smooth_kernel(block, lev, x, ke, kw, kn, de, dw, dn, *rest):
    if len(rest) == 8:
        gain, out, va, vb, fe, fw, fn, dd = rest
    else:
        gain = None
        out, va, vb, fe, fw, fn, dd = rest
    channels, rows, tiles, lanes = x.shape

    blocks = rows // block
    zero = jnp.zeros((tiles, lanes), jnp.float32)
    for c in range(channels):
        va[c, 0] = zero
        vb[c, 0] = zero
        va[c, rows + 1] = zero
        vb[c, rows + 1] = zero
        fn[c, 0] = zero

    def build(i, carry):
        c = i // blocks
        r = (i % blocks) * block
        here = pl.ds(r, block)
        level = lev[c]
        east = jnp.where(de[here] > level, ke[here], 0.0)
        west = jnp.where(dw[here] > level, kw[here], 0.0)
        north = jnp.where(dn[here] > level, kn[here], 0.0)
        fe[c, here] = east
        fw[c, here] = west
        fn[c, pl.ds(r + 1, block)] = north
        south = fn[c, here]
        dd[c, here] = 1.0 - (east + west + north + south)
        cells = x[c, here]
        if gain is not None:
            cells = cells * gain[c, here]
        va[c, pl.ds(r + 1, block)] = cells
        return carry

    lax.fori_loop(0, channels * blocks, build, 0)
    lane = lax.broadcasted_iota(jnp.int32, (block, tiles, lanes), 2)

    def step(src, dst, shift):
        def body(i, carry):
            c = i // blocks
            r = (i % blocks) * block
            here = pl.ds(r, block)
            centre = src[c, pl.ds(r + 1, block)]
            east = jnp.where(lane == 0, pltpu.roll(centre, tiles - 1, 1), centre)
            east = pltpu.roll(east, lanes - 1, 2)
            west = jnp.where(lane == lanes - 1, pltpu.roll(centre, 1, 1), centre)
            west = pltpu.roll(west, 1, 2)
            new = dd[c, here] * centre + fe[c, here] * east + fw[c, here] * west
            new = new + fn[c, pl.ds(r + 1, block)] * src[c, pl.ds(r + 2, block)]
            new = new + fn[c, here] * src[c, here]
            dst[c, pl.ds(r + shift, block)] = new
            return carry

        lax.fori_loop(0, channels * blocks, body, 0)

    step(va, vb, 1)
    step(vb, va, 1)
    step(va, vb, 1)
    step(vb, va, 1)
    step(va, out, 0)


def smooth_five(x, faces, lev, gain=None):
    channels, rows, tiles, lanes = x.shape
    vmem = pl.BlockSpec(memory_space=pltpu.VMEM)
    operands = [lev, x, *faces] + ([] if gain is None else [gain])
    field = pltpu.VMEM((channels, rows, tiles, lanes), jnp.float32)
    padded = pltpu.VMEM((channels, rows + 2, tiles, lanes), jnp.float32)
    cells = channels * rows * tiles * lanes
    return pl.pallas_call(
        functools.partial(smooth_kernel, BLOCK),
        out_shape=jax.ShapeDtypeStruct(x.shape, jnp.float32),
        in_specs=[pl.BlockSpec(memory_space=pltpu.SMEM)] + [vmem] * (len(operands) - 1),
        out_specs=vmem,
        scratch_shapes=[padded, padded, field, field, padded, field],
        cost_estimate=pl.CostEstimate(
            flops=60 * cells, bytes_accessed=16 * cells, transcendentals=0
        ),
        compiler_params=pltpu.CompilerParams(vmem_limit_bytes=48 * 1024 * 1024),
        name="smooth_five",
    )(*operands)


def local(
    kappa_east, kappa_north, depth, sigma, obs_precision, obs_tile, obs_col, obs_lat, innovation
):
    rows, lanes = kappa_east.shape
    total = sigma.shape[0]
    tiles = lax.axis_size("lon")
    bands = lax.axis_size("lat")
    devices = tiles * bands
    channels = -(-total // devices)
    listed = obs_col.shape[0]
    spare = channels * devices - total

    obs_lon = obs_tile[:, 0] * lanes + obs_col
    packed = jnp.concatenate(
        [
            kappa_east.reshape(-1),
            kappa_north.reshape(-1),
            depth.astype(jnp.float32).reshape(-1),
            obs_lon.astype(jnp.float32),
            obs_lat.astype(jnp.float32),
        ]
    ).reshape(-1, lanes)
    misfit = jnp.pad(obs_precision[:, None] * innovation, ((0, spare), (0, 0)))
    misfit = misfit.reshape(devices, channels, listed)
    sent = jnp.concatenate(
        [jnp.broadcast_to(packed[None], (devices,) + packed.shape), misfit], axis=1
    )
    everywhere = lax.all_to_all(sent, AXES, split_axis=0, concat_axis=0, tiled=True)
    misfit = everywhere[:, packed.shape[0] :]
    everywhere = everywhere[:, : packed.shape[0]]
    maps = everywhere[:, : 3 * rows].reshape(tiles, bands, 3, rows, lanes)
    maps = maps.transpose(2, 1, 3, 0, 4).reshape(3, bands * rows, tiles, lanes)
    places = everywhere[:, 3 * rows :].reshape(tiles, bands, 2, listed)
    places = places.transpose(2, 1, 0, 3).reshape(2, bands, tiles * listed)

    misfit = misfit.reshape(tiles, bands, channels, listed).transpose(1, 2, 0, 3)
    misfit = misfit.reshape(bands, channels, tiles * listed)

    me = lax.axis_index("lon") * bands + lax.axis_index("lat")
    first = me * channels
    ids = first + jnp.arange(channels, dtype=jnp.int32)
    lev = jnp.where(ids < 2 * NZ, ids % NZ, 0).astype(jnp.float32)
    scale = lax.dynamic_slice(jnp.pad(sigma, (0, spare)), (first,), (channels,))
    weight = lax.dynamic_slice(jnp.pad(obs_precision, (0, spare)), (first,), (channels,))

    height = bands * rows
    ke, kn, deep = maps[0], maps[1], maps[2]

    def shifted(field, by):
        flat = field.reshape(height, tiles * lanes)
        return jnp.roll(flat, by, 1).reshape(field.shape)

    kept = (jnp.arange(height) < height - 1)[:, None, None]
    kn = jnp.where(kept, kn, 0.0)
    de = jnp.minimum(deep, shifted(deep, -1))
    faces = (
        ke,
        shifted(ke, 1),
        kn,
        de,
        shifted(de, 1),
        jnp.minimum(deep, jnp.roll(deep, -1, 0)),
    )

    values = jnp.concatenate([misfit, jnp.ones_like(misfit[:, :1])], axis=1)
    high = lax.reduce_precision(values, 8, 7)
    left = values - high
    middle = lax.reduce_precision(left, 8, 7)
    low = left - middle
    parts = jnp.stack([high, middle, low], axis=1).astype(jnp.bfloat16)
    at_row = places[1][:, None, :] == jnp.arange(rows, dtype=jnp.float32)[None, :, None]
    at_col = (
        places[0][:, None, :] == jnp.arange(tiles * lanes, dtype=jnp.float32)[None, :, None]
    )
    spread = jnp.where(at_row[:, None, None], parts[:, :, :, None, :], 0)
    spread = spread.reshape(bands, 3 * (channels + 1) * rows, tiles * listed)
    cells = lax.dot_general(
        spread,
        at_col.astype(jnp.bfloat16),
        (((2,), (2,)), ((0,), (0,))),
        preferred_element_type=jnp.float32,
    )
    cells = cells.reshape(bands, 3, channels + 1, rows, tiles, lanes).sum(1)
    cells = cells.transpose(1, 0, 2, 3, 4).reshape(channels + 1, height, tiles, lanes)
    wet = (deep[None] > lev[:, None, None, None]).astype(jnp.float32)
    scaled_wet = scale[:, None, None, None] * wet
    gain = scaled_wet * (scale * weight)[:, None, None, None] * cells[channels][None]

    def everyone(partial):
        wide = jnp.broadcast_to(partial[None, ..., None], (devices,) + partial.shape + (lanes,))
        return lax.all_to_all(wide, AXES, split_axis=0, concat_axis=0, tiled=True).sum(0)[..., 0]

    rhs = smooth_five(scaled_wet * cells[:channels], faces, lev)
    q_one = smooth_five(rhs, faces, lev)
    sums = everyone(
        jnp.stack([jnp.sum(rhs * rhs), jnp.sum(q_one * q_one * gain)])
    )
    s_one = smooth_five(q_one, faces, lev, gain)
    norm_zero = sums[0]
    alpha_one = norm_zero / (norm_zero + sums[1])
    r_one = rhs - alpha_one * (rhs + s_one)
    norm_one = everyone(jnp.sum(r_one * r_one))
    t_one = smooth_five(r_one, faces, lev)
    beta = norm_one / norm_zero
    p_two = r_one + beta * rhs
    q_two = t_one + beta * q_one
    curve = everyone(jnp.sum(p_two * p_two + q_two * q_two * gain))
    s_two = smooth_five(q_two, faces, lev, gain)
    alpha_two = norm_one / curve

    def home(field):
        split = field.reshape(channels, bands, rows, tiles, lanes).transpose(3, 1, 0, 2, 4)
        split = split.reshape(devices, channels, rows, lanes)
        moved = lax.all_to_all(split, AXES, split_axis=0, concat_axis=0, tiled=True)
        return moved.reshape(devices * channels, rows, lanes)[:total]

    increment = home(alpha_one * rhs + alpha_two * p_two)
    residual = home(r_one - alpha_two * (p_two + s_two))
    return increment, residual


def solution(mesh):
    return jax.shard_map(
        local,
        mesh=mesh,
        in_specs=(
            P("lat", "lon"),
            P("lat", "lon"),
            P("lat", "lon"),
            P(),
            P(),
            P(("lon", "lat"), None),
            P(("lon", "lat")),
            P(("lon", "lat")),
            P(None, ("lon", "lat")),
        ),
        out_specs=(P(None, "lat", "lon"), P(None, "lat", "lon")),
        check_vma=False,
    )
```

```python
import functools

import jax
import jax.numpy as jnp
from jax import lax
from jax.experimental import pallas as pl
from jax.experimental.pallas import tpu as pltpu
from jax.sharding import PartitionSpec as P

NZ = 75
AXES = ("lon", "lat")


def smooth_kernel(stage, lev, scalar, ke, kw, kn, de, dw, dn, *rest):
    counts = {"first": 1, "curve": 2, "next": 4, "last": 3}
    fields, rest = rest[: counts[stage]], rest[counts[stage] :]
    outs, (va, vb, fe, fw, fn, dd) = rest[:-6], rest[-6:]
    channels, rows, tiles, lanes = fields[0].shape
    zero = jnp.zeros((tiles, lanes), jnp.float32)
    inner = pl.ds(1, rows)
    for c in range(channels):
        va[c, 0] = zero
        vb[c, 0] = zero
        va[c, rows + 1] = zero
        vb[c, rows + 1] = zero
        fn[c, 0] = zero

    def build(c, carry):
        level = lev[c]
        east = jnp.where(de[...] > level, ke[...], 0.0)
        west = jnp.where(dw[...] > level, kw[...], 0.0)
        north = jnp.where(dn[...] > level, kn[...], 0.0)
        fe[c] = east
        fw[c] = west
        fn[c, inner] = north
        south = fn[c, pl.ds(0, rows)]
        dd[c] = 1.0 - (east + west + north + south)
        return carry

    lax.fori_loop(0, channels, build, 0)
    lane = lax.broadcasted_iota(jnp.int32, (rows, tiles, lanes), 2)

    def step(src, dst, shift):
        def body(c, carry):
            centre = src[c, inner]
            east = jnp.where(lane == 0, pltpu.roll(centre, tiles - 1, 1), centre)
            east = pltpu.roll(east, lanes - 1, 2)
            west = jnp.where(lane == lanes - 1, pltpu.roll(centre, 1, 1), centre)
            west = pltpu.roll(west, 1, 2)
            new = dd[c] * centre + fe[c] * east + fw[c] * west
            new = new + fn[c, inner] * src[c, pl.ds(2, rows)]
            new = new + fn[c, pl.ds(0, rows)] * src[c, pl.ds(0, rows)]
            dst[c, pl.ds(shift, rows)] = new
            return carry

        lax.fori_loop(0, channels, body, 0)

    def five(dst):
        step(va, vb, 1)
        step(vb, va, 1)
        step(va, vb, 1)
        step(vb, va, 1)
        step(va, dst, 0)

    def each(body, sums):
        start = (zero,) * sums
        return lax.fori_loop(0, channels, body, start)

    if stage == "first":
        (x,) = fields
        (out,) = outs

        def load(c, carry):
            va[c, inner] = x[c]
            return carry

        each(load, 0)
        five(out)
    elif stage == "curve":
        rhs, gain = fields
        q_out, s_out, sums = outs

        def load(c, carry):
            cells = rhs[c]
            va[c, inner] = cells
            return (carry[0] + jnp.sum(cells * cells, 0),)

        (sums[0],) = each(load, 1)
        five(q_out)

        def weigh(c, carry):
            cells = q_out[c]
            gained = cells * gain[c]
            va[c, inner] = gained
            return (carry[0] + jnp.sum(cells * gained, 0),)

        (sums[1],) = each(weigh, 1)
        five(s_out)
    elif stage == "next":
        rhs, q_one, s_one, gain = fields
        r_out, t_out, sums = outs

        def load(c, carry):
            base = rhs[c]
            cells = base - scalar[0] * (base + s_one[c])
            va[c, inner] = cells
            r_out[c] = cells
            return (carry[0] + jnp.sum(cells * cells, 0), carry[1] + jnp.sum(cells * base, 0))

        sums[0], sums[1] = each(load, 2)
        five(t_out)

        def weigh(c, carry):
            cells = t_out[c]
            gained = cells * gain[c]
            return (
                carry[0] + jnp.sum(cells * gained, 0),
                carry[1] + jnp.sum(q_one[c] * gained, 0),
            )

        sums[2], sums[3] = each(weigh, 2)
    else:
        q_one, t_one, gain = fields
        (out,) = outs

        def load(c, carry):
            va[c, inner] = (t_one[c] + scalar[0] * q_one[c]) * gain[c]
            return carry

        each(load, 0)
        five(out)


def smooth(stage, lev, scalar, faces, *fields):
    channels, rows, tiles, lanes = fields[0].shape
    vmem = pl.BlockSpec(memory_space=pltpu.VMEM)
    smem = pl.BlockSpec(memory_space=pltpu.SMEM)
    outs, sums, rounds = {
        "first": (1, 0, 1),
        "curve": (2, 2, 2),
        "next": (2, 4, 1),
        "last": (1, 0, 1),
    }[stage]
    shapes = [jax.ShapeDtypeStruct(fields[0].shape, jnp.float32)] * outs
    if sums:
        shapes.append(jax.ShapeDtypeStruct((sums, tiles, lanes), jnp.float32))
    field = pltpu.VMEM((channels, rows, tiles, lanes), jnp.float32)
    padded = pltpu.VMEM((channels, rows + 2, tiles, lanes), jnp.float32)
    cells = channels * rows * tiles * lanes
    return pl.pallas_call(
        functools.partial(smooth_kernel, stage),
        out_shape=shapes,
        in_specs=[smem, smem] + [vmem] * (len(faces) + len(fields)),
        out_specs=[vmem] * len(shapes),
        scratch_shapes=[padded, padded, field, field, padded, field],
        cost_estimate=pl.CostEstimate(
            flops=60 * cells * rounds, bytes_accessed=16 * cells, transcendentals=0
        ),
        compiler_params=pltpu.CompilerParams(vmem_limit_bytes=48 * 1024 * 1024),
        name="smooth_" + stage,
    )(lev, jnp.reshape(scalar, (1,)), *faces, *fields)


def gather_kernel(reduce, tiles, bands, x, out, held, send, recv, own_sem):
    lon, lat = lax.axis_index("lon"), lax.axis_index("lat")
    beside = [(lon, lax.rem(lat + k, bands)) for k in range(1, bands)]
    along = [(lax.rem(lon + k, tiles), lat) for k in range(1, tiles)]
    barrier = pltpu.get_barrier_semaphore()
    for peer in beside + along:
        pl.semaphore_signal(
            barrier, inc=1, device_id=peer, device_id_type=pl.DeviceIdType.MESH
        )
    pl.semaphore_wait(barrier, len(beside) + len(along))

    def post(source, target, peer, number):
        copy = pltpu.make_async_remote_copy(
            src_ref=source,
            dst_ref=target,
            send_sem=send.at[number],
            recv_sem=recv.at[number],
            device_id=peer,
            device_id_type=pl.DeviceIdType.MESH,
        )
        copy.start()
        return copy

    copies = [post(x, held.at[lon, lat], peer, k) for k, peer in enumerate(beside)]
    own = pltpu.make_async_copy(x, held.at[lon, lat], own_sem)
    own.start()
    own.wait()
    for copy in copies:
        copy.wait()
    copies = [
        post(held.at[lon], held.at[lon], peer, len(beside) + k) for k, peer in enumerate(along)
    ]
    for copy in copies:
        copy.wait()
    if reduce:
        out[...] = jnp.sum(held[...], (0, 1))
    else:
        out[...] = held[...]


def gather(x, reduce, number):
    tiles = lax.axis_size("lon")
    bands = lax.axis_size("lat")
    full = (tiles, bands) + x.shape
    vmem = pl.BlockSpec(memory_space=pltpu.VMEM)
    peers = tiles + bands - 2
    return pl.pallas_call(
        functools.partial(gather_kernel, reduce, tiles, bands),
        out_shape=jax.ShapeDtypeStruct(x.shape if reduce else full, jnp.float32),
        in_specs=[vmem],
        out_specs=vmem,
        scratch_shapes=[
            pltpu.VMEM(full, jnp.float32),
            pltpu.SemaphoreType.DMA((peers,)),
            pltpu.SemaphoreType.DMA((peers,)),
            pltpu.SemaphoreType.DMA,
        ],
        cost_estimate=pl.CostEstimate(
            flops=0, bytes_accessed=20_000_000, transcendentals=0
        ),
        compiler_params=pltpu.CompilerParams(
            collective_id=number, has_side_effects=True, vmem_limit_bytes=24 * 1024 * 1024
        ),
        name=f"gather_{number}",
    )(x)


def local(
    kappa_east, kappa_north, depth, sigma, obs_precision, obs_tile, obs_col, obs_lat, innovation
):
    rows, lanes = kappa_east.shape
    total = sigma.shape[0]
    tiles = lax.axis_size("lon")
    bands = lax.axis_size("lat")
    devices = tiles * bands
    channels = -(-total // devices)
    listed = obs_col.shape[0]
    spare = channels * devices - total

    obs_lon = obs_tile[:, 0] * lanes + obs_col
    packed = jnp.concatenate(
        [
            kappa_east.reshape(-1),
            kappa_north.reshape(-1),
            depth.astype(jnp.float32).reshape(-1),
            obs_lon.astype(jnp.float32),
            obs_lat.astype(jnp.float32),
        ]
    ).reshape(-1, lanes)
    misfit = jnp.pad(obs_precision[:, None] * innovation, ((0, spare), (0, 0)))
    misfit = misfit.reshape(devices, channels, listed)
    misfit = lax.all_to_all(misfit, AXES, split_axis=0, concat_axis=0, tiled=True)
    packed = jnp.pad(packed, ((0, -packed.shape[0] % 8), (0, 0)))
    everywhere = gather(packed, False, 1)
    everywhere = everywhere.reshape((devices,) + packed.shape)
    used = 3 * rows + 2 * listed // lanes
    maps = everywhere[:, : 3 * rows].reshape(tiles, bands, 3, rows, lanes)
    maps = maps.transpose(2, 1, 3, 0, 4).reshape(3, bands * rows, tiles, lanes)
    places = everywhere[:, 3 * rows : used].reshape(tiles, bands, 2, listed)
    places = places.transpose(2, 1, 0, 3).reshape(2, bands, tiles * listed)
    misfit = misfit.reshape(tiles, bands, channels, listed).transpose(1, 2, 0, 3)
    misfit = misfit.reshape(bands, channels, tiles * listed)

    me = lax.axis_index("lon") * bands + lax.axis_index("lat")
    first = me * channels
    ids = first + jnp.arange(channels, dtype=jnp.int32)
    lev = jnp.where(ids < 2 * NZ, ids % NZ, 0).astype(jnp.float32)
    scale = lax.dynamic_slice(jnp.pad(sigma, (0, spare)), (first,), (channels,))
    weight = lax.dynamic_slice(jnp.pad(obs_precision, (0, spare)), (first,), (channels,))

    height = bands * rows
    ke, kn, deep = maps[0], maps[1], maps[2]

    def shifted(field, by):
        flat = field.reshape(height, tiles * lanes)
        return jnp.roll(flat, by, 1).reshape(field.shape)

    kept = (jnp.arange(height) < height - 1)[:, None, None]
    kn = jnp.where(kept, kn, 0.0)
    de = jnp.minimum(deep, shifted(deep, -1))
    faces = (
        ke,
        shifted(ke, 1),
        kn,
        de,
        shifted(de, 1),
        jnp.minimum(deep, jnp.roll(deep, -1, 0)),
    )

    values = jnp.concatenate([misfit, jnp.ones_like(misfit[:, :1])], axis=1)
    high = lax.reduce_precision(values, 8, 7)
    left = values - high
    middle = lax.reduce_precision(left, 8, 7)
    low = left - middle
    parts = jnp.stack([high, middle, low], axis=1).astype(jnp.bfloat16)
    at_row = places[1][:, None, :] == jnp.arange(rows, dtype=jnp.float32)[None, :, None]
    at_col = (
        places[0][:, None, :] == jnp.arange(tiles * lanes, dtype=jnp.float32)[None, :, None]
    )
    spread = jnp.where(at_row[:, None, None], parts[:, :, :, None, :], 0)
    spread = spread.reshape(bands, 3 * (channels + 1) * rows, tiles * listed)
    cells = lax.dot_general(
        spread,
        at_col.astype(jnp.bfloat16),
        (((2,), (2,)), ((0,), (0,))),
        preferred_element_type=jnp.float32,
    )
    cells = cells.reshape(bands, 3, channels + 1, rows, tiles, lanes).sum(1)
    cells = cells.transpose(1, 0, 2, 3, 4).reshape(channels + 1, height, tiles, lanes)
    wet = (deep[None] > lev[:, None, None, None]).astype(jnp.float32)
    scaled_wet = scale[:, None, None, None] * wet
    gain = scaled_wet * (scale * weight)[:, None, None, None] * cells[channels][None]

    def everyone(sums, number):
        partial = jnp.pad(jnp.sum(sums, 1), ((0, 8 - sums.shape[0]), (0, 0)))
        return jnp.sum(gather(partial, True, number), 1)

    def home(field):
        split = field.reshape(channels, bands, rows, tiles, lanes).transpose(3, 1, 0, 2, 4)
        split = split.reshape(devices, channels, rows, lanes)
        moved = lax.all_to_all(split, AXES, split_axis=0, concat_axis=0, tiled=True)
        return moved.reshape(devices * channels, rows, lanes)[:total]

    none = jnp.float32(0.0)
    (rhs,) = smooth("first", lev, none, faces, scaled_wet * cells[:channels])
    rhs_home = home(rhs)
    q_one, s_one, sums = smooth("curve", lev, none, faces, rhs, gain)
    sums = everyone(sums, 2)
    norm_zero, bend = sums[0], sums[1]
    alpha_one = norm_zero / (norm_zero + bend)
    r_one, t_one, sums = smooth("next", lev, alpha_one, faces, rhs, q_one, s_one, gain)
    sums, rhs_home = lax.optimization_barrier((sums, rhs_home))
    r_home = home(r_one)
    sums = everyone(sums, 3)
    norm_one = sums[0]
    beta = norm_one / norm_zero
    curve = (
        norm_one
        + sums[2]
        + 2.0 * beta * (sums[1] + sums[3])
        + beta * beta * (norm_zero + bend)
    )
    alpha_two = norm_one / curve
    (s_two,) = smooth("last", lev, beta, faces, q_one, t_one, gain)
    p_home = r_home + beta * rhs_home
    increment = alpha_one * rhs_home + alpha_two * p_home
    residual = r_home - alpha_two * (p_home + home(s_two))
    return increment, residual


def solution(mesh):
    return jax.shard_map(
        local,
        mesh=mesh,
        in_specs=(
            P("lat", "lon"),
            P("lat", "lon"),
            P("lat", "lon"),
            P(),
            P(),
            P(("lon", "lat"), None),
            P(("lon", "lat")),
            P(("lon", "lat")),
            P(None, ("lon", "lat")),
        ),
        out_specs=(P(None, "lat", "lon"), P(None, "lat", "lon")),
        check_vma=False,
    )
```
